256 devices in a mesh: layer: 8 (over y, core), unit: 32 (over x, z).
Axes of the slice: x: 4, y: 4, z: 8, core: 2. Of those that a mesh axis runs over, the one named last changes fastest.
Arguments:
- tokens: int32 [4, 32], replicated, may hold values from 0 to 255
- embed: bfloat16 [256, 8192], P(None, 'unit'), may hold values from -6 to 6
- weights: bfloat16 [8, 128, 32, 64, 256], P('layer', 'unit'), may hold values from -0.125 to 0.125
- layout: int32 [8, 128, 32], P('layer', 'unit'), may hold values from 0 to 255, as said below
- bias: float32 [8, 128, 256], P('layer', 'unit'), may hold values from -4 to 4
- d_hidden: bfloat16 [8, 4, 32, 8192], P('layer', None, None, 'unit'), may hold values from -6 to 6
Outputs:
- hidden: bfloat16 [8, 4, 32, 8192], P('layer', None, None, 'unit')
- grad_weights: bfloat16 [8, 128, 32, 64, 256], P('layer', 'unit')
- grad_bias: float32 [8, 128, 256], P('layer', 'unit')
The draws below stay inside these ranges and needn't reach their ends.
Inputs may be any that keep to these rules, and one draw needn't show every extreme that they name: The 32 entries of every row layout[l, j] are distinct and rising; numbers under 128 are blocks of the layer's input, the others of its own previous hidden state.
All inputs are finite; a program needn't handle non-finite values.
Results may differ from the reference program's by a relative error of at most 0.0085.
Values may be sent and summed in bfloat16 or wider, within the bound.
No kernel may reach another device: no remote copies, remote signals or barrier semaphores. Data moves between devices by JAX's collectives and lax.ppermute only.
A program may use at most 64 MiB of HBM per device.

```python
import jax
import jax.numpy as jnp
from jax import lax

H = 8192
BLK = 64
VOCAB = 256
B = 32
STEPS = 4
HB = 128
NNZ = 32
LAYERS = 8
N_UNIT = 32


def draw_layout(key, part):
    scores = jax.random.randint(key, (LAYERS, HB, 2 * HB), 0, 1 << 20) * (2 * HB) + jnp.arange(2 * HB, dtype=jnp.int32)
    chosen = lax.top_k(scores, NNZ)[1]
    return jnp.sort(chosen, axis=-1).astype(jnp.int32)


def place_ends(array, stream_key, low, top_value):
    extent = array.shape
    spot = [jax.random.randint(jax.random.fold_in(stream_key, axis), (), 0, extent[axis]) for axis in range(len(extent))]
    array = array.at[tuple(spot)].set(low)
    longest = extent.index(max(extent))
    spot[longest] = (spot[longest] + 1) % extent[longest]
    return array.at[tuple(spot)].set(top_value)


def steps_of(key, extent, split, smallest, largest):
    def one(position, blocks):
        draws = jax.random.uniform(jax.random.fold_in(jax.random.fold_in(key, 6), position), (blocks,), jnp.float32, smallest / len(split), largest / len(split))
        return jnp.repeat(jnp.exp(draws), extent[position] // blocks).reshape((-1,) + (1,) * (len(extent) - position - 1))

    gain = one(*split[0])
    for cut in split[1:]:
        gain = gain * one(*cut)
    return gain


def scatter_about(rng, shape, scale, bound, pieces=(), kind=jnp.bfloat16):
    level = steps_of(rng, shape, pieces, -0.22, 0.18) if pieces else 1.0
    values = jax.random.normal(rng, shape, jnp.float32) * scale * level
    return jnp.minimum(jnp.maximum(values, -bound), bound).astype(kind)


def setup_inputs(seed: int = 0) -> dict:
    arg_keys = jax.random.split(jax.random.key(seed), 7)
    return {
        "tokens": place_ends(jax.random.randint(arg_keys[0], (STEPS, B), 0, VOCAB), jax.random.fold_in(arg_keys[0], 1), 0, VOCAB - 1).astype(jnp.int32),
        "embed": scatter_about(arg_keys[1], (VOCAB, H), 1.0, 6.0, ((1, 32),)),
        "weights": scatter_about(arg_keys[2], (LAYERS, HB, NNZ, BLK, 4 * BLK), (NNZ * BLK) ** -0.5, 0.125, ((0, 8), (1, 32))),
        "layout": draw_layout(jax.random.fold_in(arg_keys[6], 71), 0),
        "bias": scatter_about(arg_keys[4], (LAYERS, HB, 4 * BLK), 1.0, 4.0, ((0, 8), (1, 32)), jnp.float32),
        "d_hidden": scatter_about(arg_keys[5], (LAYERS, STEPS, B, H), 1.0, 6.0, ((0, 8), (3, 32))),
    }


def gate_math(pre_act, cell_prev):
    gate_size = pre_act.shape[-1] // 4
    in_gate = jax.nn.sigmoid(pre_act[..., :gate_size])
    forget = jax.nn.sigmoid(pre_act[..., gate_size:2 * gate_size])
    update = jnp.tanh(pre_act[..., 2 * gate_size:3 * gate_size])
    out_gate = jax.nn.sigmoid(pre_act[..., 3 * gate_size:])
    cell_state = forget * cell_prev + in_gate * update
    new_hidden = (out_gate * jnp.tanh(cell_state)).astype(jnp.bfloat16)
    return jnp.concatenate([in_gate, forget, update, out_gate], -1), cell_state, new_hidden


def gate_grads(gate_acts, cell_state, cell_prev, grad_hidden, grad_carry):
    gate_size = gate_acts.shape[-1] // 4
    in_gate = gate_acts[..., :gate_size]
    forget = gate_acts[..., gate_size:2 * gate_size]
    update = gate_acts[..., 2 * gate_size:3 * gate_size]
    out_gate = gate_acts[..., 3 * gate_size:]
    squash = jnp.tanh(cell_state)
    grad_cell = grad_carry + grad_hidden * out_gate * (1.0 - squash * squash)
    grad_in = grad_cell * update * in_gate * (1.0 - in_gate)
    grad_forget = grad_cell * cell_prev * forget * (1.0 - forget)
    grad_update = grad_cell * in_gate * (1.0 - update * update)
    grad_out = grad_hidden * squash * out_gate * (1.0 - out_gate)
    grad_pre = jnp.concatenate([grad_in, grad_forget, grad_update, grad_out], -1).astype(jnp.bfloat16)
    return grad_pre, grad_cell * forget


def sparse_product(inputs, weight_f, layout_rows):
    picked = jnp.take(inputs, layout_rows, axis=1).astype(jnp.float32)
    return jnp.einsum("bjkc,jkcd->bjd", picked, weight_f)


def spread(grad_pre, weight_f, layout_rows):
    batch_rows = grad_pre.shape[0]
    group_size = HB // N_UNIT
    contrib = jnp.einsum("bjd,jkcd->bjkc", grad_pre.astype(jnp.float32), weight_f)
    contrib = contrib.reshape(batch_rows, N_UNIT, group_size * NNZ, BLK)
    index_rows = layout_rows.reshape(N_UNIT, group_size * NNZ)

    def one_group(piece, index_row):
        return jnp.zeros((batch_rows, 2 * HB, BLK), jnp.float32).at[:, index_row].add(piece)

    parts = jax.vmap(one_group, in_axes=(1, 0))(contrib, index_rows)
    rounded = lax.optimization_barrier(parts.astype(jnp.bfloat16)).astype(jnp.float32)
    return jnp.sum(rounded, 0).reshape(batch_rows, 2 * H)


def reference(tokens, embed, weights, layout, bias, d_hidden):
    source = jnp.take(embed, tokens, axis=0)
    saved = []
    hidden_all = []
    for layer_idx in range(LAYERS):
        weight_f = weights[layer_idx].astype(jnp.float32)
        layout_rows = layout[layer_idx]
        bias_rows = bias[layer_idx]

        def advance(loop_state, source_row):
            hidden_prev, cell_prev = loop_state
            inputs = jnp.concatenate([source_row, hidden_prev], -1).reshape(B, 2 * HB, BLK)
            pre_act = sparse_product(inputs, weight_f, layout_rows) + bias_rows
            gate_acts, cell_state, new_hidden = gate_math(pre_act, cell_prev)
            new_hidden = new_hidden.reshape(B, H)
            return (new_hidden, cell_state), (new_hidden, cell_state, gate_acts, inputs)

        start = (jnp.zeros((B, H), jnp.bfloat16), jnp.zeros((B, HB, BLK), jnp.float32))
        _, (hidden_seq, cell_seq, act_seq, input_seq) = lax.scan(advance, start, source)
        saved.append((cell_seq, act_seq, input_seq))
        hidden_all.append(hidden_seq)
        source = hidden_seq
    from_above = jnp.zeros((STEPS, B, H), jnp.float32)
    grad_w_all = [None] * LAYERS
    grad_b_all = [None] * LAYERS
    for layer_idx in reversed(range(LAYERS)):
        weight_f = weights[layer_idx].astype(jnp.float32)
        layout_rows = layout[layer_idx]
        cell_seq, act_seq, input_seq = saved[layer_idx]
        prev_seq = jnp.concatenate([jnp.zeros((1, B, HB, BLK), jnp.float32), cell_seq[:-1]], 0)

        def retreat(loop_state, row_items):
            grad_recur, grad_carry = loop_state
            upstream, above, gate_acts, cell_state, cell_prev = row_items
            grad_hidden = upstream.astype(jnp.float32) + above + grad_recur
            grad_pre, carry_new = gate_grads(gate_acts, cell_state, cell_prev, grad_hidden.reshape(B, HB, BLK), grad_carry)
            partial_value = spread(grad_pre, weight_f, layout_rows)
            return (partial_value[:, H:], carry_new), (grad_pre, partial_value[:, :H])

        start = (jnp.zeros((B, H), jnp.float32), jnp.zeros((B, HB, BLK), jnp.float32))
        rows_in = (d_hidden[layer_idx], from_above, act_seq, cell_seq, prev_seq)
        _, (pre_seq, down_seq) = lax.scan(retreat, start, rows_in, reverse=True)
        picked_all = jnp.take(input_seq, layout_rows, axis=2).astype(jnp.float32)
        grad_w = jnp.einsum("sbjkc,sbjd->jkcd", picked_all, pre_seq.astype(jnp.float32))
        grad_w_all[layer_idx] = grad_w.astype(jnp.bfloat16)
        grad_b_all[layer_idx] = jnp.sum(pre_seq.astype(jnp.float32), axis=(0, 1))
        from_above = down_seq
    return jnp.stack(hidden_all, 0), jnp.stack(grad_w_all, 0), jnp.stack(grad_b_all, 0)
```

```python
import jax
import jax.numpy as jnp
from jax import lax
from jax.experimental import pallas as pl
from jax.experimental.pallas import tpu as pltpu
from jax.sharding import Mesh
from jax.sharding import PartitionSpec as P

UNIT = ("unit_0", "unit_1")
STREAMS = 1
LANES = 128
F32 = jnp.float32
BF16 = jnp.bfloat16


def dot(lhs, rhs, dims):
    return lax.dot_general(lhs, rhs, (dims, ((), ())), preferred_element_type=F32)


def turned(value):
    return pltpu.roll(value.astype(F32), LANES // 2, 1)


def forward_kernel(nnz, blk, half_chunks, copies):
    def body(
        layout_ref, meta_ref, src_ref, hid_ref, w_ref, bias_ref, extra_ref, cell_in,
        _a, _b, _c, picked_ref, act_ref, cell_ref, hlog_ref, send_ref, hid_s,
    ):
        j = pl.program_id(0)
        own = hid_s.shape[0]
        active = meta_ref[0] > 0
        started = meta_ref[3] > 0
        rows = src_ref.shape[1]
        upper = lax.broadcasted_iota(jnp.int32, (rows, LANES), 1) >= blk

        def block(index, half):
            number = layout_ref[j * nnz + index]
            chunk = number // 2
            value = jnp.where(
                chunk < half_chunks,
                src_ref[jnp.minimum(chunk, half_chunks - 1)],
                hid_ref[jnp.maximum(chunk - half_chunks, 0)],
            ).astype(F32)
            return jnp.where(number % 2 == half, value, pltpu.roll(value, blk, 1))

        for pair in range(nnz // 2):
            both = jnp.where(upper, block(2 * pair + 1, 1), block(2 * pair, 0))
            picked_ref[0, 0, :, pair * LANES : (pair + 1) * LANES] = both.astype(BF16)
        pre_act = dot(picked_ref[0, 0], w_ref[0], ((1,), (0,))) + bias_ref[0]
        gates = jax.nn.sigmoid(pre_act)
        update = jnp.tanh(pre_act[:, 2 * blk : 3 * blk])
        cell_prev = jnp.where(started, cell_in[0, 0], 0.0)
        cell = gates[:, blk : 2 * blk] * cell_prev + gates[:, :blk] * update
        act_ref[0, 0] = jnp.concatenate([gates[:, : 2 * blk], update, gates[:, 3 * blk :]], 1)
        cell_ref[0, 0] = cell
        hid_s[j] = jnp.where(active, gates[:, 3 * blk :] * jnp.tanh(cell), 0.0)

        @pl.when(j == own - 1)
        def _():
            chunks = []
            for c in range(own // 2):
                joined = jnp.concatenate([hid_s[2 * c], hid_s[2 * c + 1]], 1).astype(BF16)
                hlog_ref[0, :, c * LANES : (c + 1) * LANES] = joined
                chunks.append(joined + extra_ref[0, :, c * LANES : (c + 1) * LANES])
            payload = jnp.concatenate(chunks, 0)
            for d in range(copies):
                send_ref[d] = payload

    return body


def forward_call(layout, meta, src, hid, w, bias, extra, picked, act, cell, hlog, copies):
    own, wide, gate_width = w.shape
    half_chunks, rows, _ = src.shape
    nnz = layout.shape[0] // own
    blk = wide // nnz
    grid_spec = pltpu.PrefetchScalarGridSpec(
        num_scalar_prefetch=2,
        grid=(own,),
        in_specs=[
            pl.BlockSpec(src.shape, lambda j, lay, m: (0, 0, 0)),
            pl.BlockSpec(hid.shape, lambda j, lay, m: (0, 0, 0)),
            pl.BlockSpec((1, wide, gate_width), lambda j, lay, m: (j, 0, 0)),
            pl.BlockSpec((1, 1, gate_width), lambda j, lay, m: (j, 0, 0)),
            pl.BlockSpec((1, *extra.shape[1:]), lambda j, lay, m: (m[4], 0, 0)),
            pl.BlockSpec((1, 1, rows, blk), lambda j, lay, m: (m[2], j, 0, 0)),
            pl.BlockSpec(memory_space=pl.ANY),
            pl.BlockSpec(memory_space=pl.ANY),
            pl.BlockSpec(memory_space=pl.ANY),
        ],
        out_specs=[
            pl.BlockSpec((1, 1, rows, wide), lambda j, lay, m: (m[1], j, 0, 0)),
            pl.BlockSpec((1, 1, rows, gate_width), lambda j, lay, m: (m[1], j, 0, 0)),
            pl.BlockSpec((1, 1, rows, blk), lambda j, lay, m: (m[1], j, 0, 0)),
            pl.BlockSpec((1, rows, own * blk), lambda j, lay, m: (m[1], 0, 0)),
            pl.BlockSpec((copies, own // 2 * rows, LANES), lambda j, lay, m: (0, 0, 0)),
        ],
        scratch_shapes=[pltpu.VMEM((own, rows, blk), F32)],
    )
    out_shape = [
        jax.ShapeDtypeStruct(picked.shape, picked.dtype),
        jax.ShapeDtypeStruct(act.shape, act.dtype),
        jax.ShapeDtypeStruct(cell.shape, cell.dtype),
        jax.ShapeDtypeStruct(hlog.shape, hlog.dtype),
        jax.ShapeDtypeStruct((copies, own // 2 * rows, LANES), BF16),
    ]
    return pl.pallas_call(
        forward_kernel(nnz, blk, half_chunks, copies),
        grid_spec=grid_spec,
        out_shape=out_shape,
        input_output_aliases={7: 2, 8: 0, 9: 1, 10: 3},
        name="forward_wave",
    )(layout, meta, src, hid, w, bias, extra, cell, picked, act, hlog)


def backward_kernel(nnz, blk, half_chunks):
    def body(
        layout_ref, meta_ref, above_ref, recur_ref, cot_ref, w_ref, act_ref, cell_ref, prev_ref,
        carry_ref, _p, pre_ref, carry_out, down_ref, back_ref, acc, grad_s,
    ):
        j = pl.program_id(0)
        own, rows, _ = grad_s.shape
        active = meta_ref[0] > 0
        later = meta_ref[3] > 0
        upper = lax.broadcasted_iota(jnp.int32, (rows, LANES), 1) >= blk

        @pl.when(j == 0)
        def _():
            acc[...] = jnp.zeros_like(acc)
            total = recur_ref[0].astype(F32)
            for d in range(1, recur_ref.shape[0]):
                total = total + recur_ref[d].astype(F32)
            for c in range(own // 2):
                piece = total[c * rows : (c + 1) * rows]
                lanes = slice(c * LANES, (c + 1) * LANES)
                piece = piece + above_ref[:, lanes].astype(F32) + cot_ref[0, :, lanes].astype(F32)
                grad_s[2 * c] = piece[:, :blk]
                grad_s[2 * c + 1] = piece[:, blk:]

        gates = act_ref[0, 0]
        in_gate = gates[:, :blk]
        forget = gates[:, blk : 2 * blk]
        update = gates[:, 2 * blk : 3 * blk]
        out_gate = gates[:, 3 * blk :]
        grad_hidden = grad_s[j]
        cell_prev = jnp.where(later, prev_ref[0, 0], 0.0)
        squash = jnp.tanh(cell_ref[0, 0])
        grad_cell = carry_ref[0] + grad_hidden * out_gate * (1.0 - squash * squash)
        grad_in = grad_cell * update * in_gate * (1.0 - in_gate)
        grad_forget = grad_cell * cell_prev * forget * (1.0 - forget)
        grad_update = grad_cell * in_gate * (1.0 - update * update)
        grad_out = grad_hidden * squash * out_gate * (1.0 - out_gate)
        grad_pre = jnp.concatenate([grad_in, grad_forget, grad_update, grad_out], 1)
        grad_pre = jnp.where(active, grad_pre, 0.0).astype(BF16)
        pre_ref[0, 0] = grad_pre
        carry_out[0] = jnp.where(active, grad_cell * forget, 0.0)
        for part in range(nnz * blk // 512):
            contrib = dot(grad_pre, w_ref[0, part * 512 : (part + 1) * 512, :], ((1,), (1,)))
            for q in range(512 // LANES):
                value = contrib[:, q * LANES : (q + 1) * LANES]
                swapped = pltpu.roll(value, blk, 1)
                for half in range(2):
                    number = layout_ref[j * nnz + part * (512 // blk) + 2 * q + half]
                    odd = number % 2
                    placed = jnp.where(odd == half, value, swapped)
                    placed = jnp.where(upper == (odd == 1), placed, 0.0)
                    acc[number // 2] += placed

        @pl.when(j == own - 1)
        def _():
            shape = down_ref.shape
            down_ref[...] = acc[:half_chunks].astype(BF16).reshape(shape)
            back_ref[...] = acc[half_chunks:].astype(BF16).reshape(shape)

    return body


def backward_call(layout, meta, above, recur, cot, w, act, cell, carry, pre):
    own, wide, gate_width = w.shape
    devices, _, _ = recur.shape
    rows = above.shape[0]
    nnz = layout.shape[0] // own
    blk = wide // nnz
    half_chunks = devices * own // 2
    sent = (devices, own // 2 * rows, LANES)
    grid_spec = pltpu.PrefetchScalarGridSpec(
        num_scalar_prefetch=2,
        grid=(own,),
        in_specs=[
            pl.BlockSpec(above.shape, lambda j, lay, m: (0, 0)),
            pl.BlockSpec(recur.shape, lambda j, lay, m: (0, 0, 0)),
            pl.BlockSpec((1, rows, own * blk), lambda j, lay, m: (m[4], 0, 0)),
            pl.BlockSpec((1, wide, gate_width), lambda j, lay, m: (j, 0, 0)),
            pl.BlockSpec((1, 1, rows, gate_width), lambda j, lay, m: (m[4], j, 0, 0)),
            pl.BlockSpec((1, 1, rows, blk), lambda j, lay, m: (m[4], j, 0, 0)),
            pl.BlockSpec((1, 1, rows, blk), lambda j, lay, m: (m[2], j, 0, 0)),
            pl.BlockSpec((1, rows, blk), lambda j, lay, m: (j, 0, 0)),
            pl.BlockSpec(memory_space=pl.ANY),
        ],
        out_specs=[
            pl.BlockSpec((1, 1, rows, gate_width), lambda j, lay, m: (m[1], j, 0, 0)),
            pl.BlockSpec((1, rows, blk), lambda j, lay, m: (j, 0, 0)),
            pl.BlockSpec(sent, lambda j, lay, m: (0, 0, 0)),
            pl.BlockSpec(sent, lambda j, lay, m: (0, 0, 0)),
        ],
        scratch_shapes=[
            pltpu.VMEM((2 * half_chunks, rows, LANES), F32),
            pltpu.VMEM((own, rows, blk), F32),
        ],
    )
    out_shape = [
        jax.ShapeDtypeStruct(pre.shape, pre.dtype),
        jax.ShapeDtypeStruct(carry.shape, carry.dtype),
        jax.ShapeDtypeStruct(sent, BF16),
        jax.ShapeDtypeStruct(sent, BF16),
    ]
    return pl.pallas_call(
        backward_kernel(nnz, blk, half_chunks),
        grid_spec=grid_spec,
        out_shape=out_shape,
        input_output_aliases={10: 0},
        name="backward_wave",
    )(layout, meta, above, recur, cot, w, act, cell, cell, carry, pre)


def total_kernel(own, rows):
    def body(parts_ref, out_ref):
        total = parts_ref[0].astype(F32)
        for d in range(1, parts_ref.shape[0]):
            total = total + parts_ref[d].astype(F32)
        for c in range(own // 2):
            out_ref[:, c * LANES : (c + 1) * LANES] = total[c * rows : (c + 1) * rows].astype(BF16)

    return body


def total_of(parts, own, rows):
    return pl.pallas_call(
        total_kernel(own, rows),
        out_shape=jax.ShapeDtypeStruct((rows, own // 2 * LANES), BF16),
        name="arrival_sum",
    )(parts)


def weight_grad_kernel(streams):
    def body(*refs):
        picked, pre = refs[:streams], refs[streams : 2 * streams]
        grad_ref, bias_ref = refs[2 * streams :]
        steps, _, rows, wide = picked[0].shape
        gate_width = pre[0].shape[-1]
        lhs = [p[...].reshape(steps * rows, wide) for p in picked]
        rhs = [p[...].reshape(steps * rows, gate_width) for p in pre]
        lhs = lhs[0] if streams == 1 else jnp.concatenate(lhs, 0)
        rhs = rhs[0] if streams == 1 else jnp.concatenate(rhs, 0)
        grad_ref[0] = dot(lhs, rhs, ((0,), (0,))).astype(BF16)
        bias_ref[0] = jnp.sum(rhs.astype(F32), 0, keepdims=True)

    return body


def weight_grads(picked, pre, steps):
    streams = len(picked)
    _, own, rows, wide = picked[0].shape
    gate_width = pre[0].shape[-1]
    return pl.pallas_call(
        weight_grad_kernel(streams),
        grid=(own,),
        in_specs=[pl.BlockSpec((steps, 1, rows, wide), lambda j: (0, j, 0, 0))] * streams
        + [pl.BlockSpec((steps, 1, rows, gate_width), lambda j: (0, j, 0, 0))] * streams,
        out_specs=[
            pl.BlockSpec((1, wide, gate_width), lambda j: (j, 0, 0)),
            pl.BlockSpec((1, 1, gate_width), lambda j: (j, 0, 0)),
        ],
        out_shape=[
            jax.ShapeDtypeStruct((own, wide, gate_width), BF16),
            jax.ShapeDtypeStruct((own, 1, gate_width), F32),
        ],
        name="weight_grads",
    )(*picked, *pre)


def exchanged(pieces):
    return lax.all_to_all(pieces, UNIT, 0, 0, tiled=True)


def on_device(tokens, embed, weights, layout, bias, d_hidden):
    layer_count = lax.axis_size("layer")
    layer_idx = lax.axis_index("layer")
    devices = lax.axis_size(UNIT)
    steps, batch = tokens.shape
    vocab, unit_width = embed.shape
    own, nnz, blk, gate_width = weights.shape[1:]
    w = weights[0].reshape(own, nnz * blk, gate_width)
    lay = layout[0].reshape(-1)
    bias_rows = bias[0].reshape(own, 1, gate_width)
    waves = steps + layer_count - 1
    rows = batch // STREAMS
    chunks = devices * own // 2
    streams = range(STREAMS)
    part = [slice(s * rows, (s + 1) * rows) for s in streams]
    cot = [d_hidden[0][:, part[s]] for s in streams]

    vocab_ids = jnp.arange(vocab, dtype=jnp.int32)
    onehot = (tokens.reshape(-1)[:, None] == vocab_ids[None, :]).astype(BF16)
    looked = dot(onehot, embed, ((1,), (0,))).astype(BF16).reshape(steps, batch, unit_width)
    is_last = layer_idx == layer_count - 1
    looked = jnp.where(is_last, looked, jnp.zeros_like(looked))
    looked = jnp.concatenate([looked, jnp.zeros((1, batch, unit_width), BF16)], 0)
    extra = [looked[:, part[s]] for s in streams]
    ring = [(src, (src + 1) % layer_count) for src in range(layer_count)]
    lower = [(src, src - 1) for src in range(1, layer_count)]

    def meta_of(time_step, extra_row):
        in_range = (time_step >= 0) & (time_step < steps)
        clipped = jnp.clip(time_step, 0, steps - 1)
        slot = jnp.where(in_range, time_step, steps)
        previous = jnp.maximum(clipped - 1, 0)
        later = in_range & (time_step > 0)
        row = clipped if extra_row is None else extra_row
        return jnp.stack(
            [in_range.astype(jnp.int32), slot, previous, later.astype(jnp.int32), row]
        ).astype(jnp.int32)

    def first_payload(s):
        wide = extra[s][0].reshape(rows, own // 2, LANES).transpose(1, 0, 2)
        flat = wide.reshape(own // 2 * rows, LANES)
        return jnp.broadcast_to(flat[None], (devices, *flat.shape))

    def forward_wave(wave, state):
        meta = meta_of(wave - layer_idx, jnp.minimum(wave + 1, steps))
        gathered = [exchanged(state[s][0]).reshape(chunks, rows, LANES) for s in streams]
        below = [lax.ppermute(g, "layer", ring) for g in gathered]
        new = []
        for s in streams:
            _, picked, act, cell, hlog = state[s]
            picked, act, cell, hlog, send = forward_call(
                lay, meta, below[s], gathered[s], w, bias_rows, extra[s],
                picked, act, cell, hlog, devices,
            )
            new.append((send, picked, act, cell, hlog))
        return tuple(new)

    start = tuple(
        (
            first_payload(s),
            jnp.zeros((steps + 1, own, rows, nnz * blk), BF16),
            jnp.zeros((steps + 1, own, rows, gate_width), F32),
            jnp.zeros((steps + 1, own, rows, blk), F32),
            jnp.zeros((steps + 1, rows, unit_width), BF16),
        )
        for s in streams
    )
    logs = lax.fori_loop(0, waves, forward_wave, start)

    def backward_wave(wave, state):
        meta = meta_of(steps - 1 - wave + (layer_count - 1 - layer_idx), None)
        new = []
        for s in streams:
            above, recur, carry, pre = state[s]
            _, _, act, cell, _ = logs[s]
            pre, carry, down, back = backward_call(
                lay, meta, above, recur, cot[s], w, act, cell, carry, pre
            )
            down = total_of(exchanged(down), own, rows)
            recur = exchanged(back)
            above = lax.ppermute(down, "layer", lower)
            new.append((above, recur, carry, pre))
        return tuple(new)

    start = tuple(
        (
            jnp.zeros((rows, unit_width), BF16),
            jnp.zeros((devices, own // 2 * rows, LANES), BF16),
            jnp.zeros((own, rows, blk), F32),
            jnp.zeros((steps + 1, own, rows, gate_width), BF16),
        )
        for s in streams
    )
    ends = lax.fori_loop(0, waves, backward_wave, start)
    grad_w, grad_b = weight_grads([logs[s][1] for s in streams], [ends[s][3] for s in streams], steps)
    hidden = [logs[s][4][:steps] for s in streams]
    hidden = hidden[0] if STREAMS == 1 else jnp.concatenate(hidden, 1)
    return (
        hidden[None],
        grad_w.reshape(1, own, nnz, blk, gate_width),
        grad_b.reshape(1, own, gate_width),
    )


def solution(mesh):
    torus = Mesh(mesh.devices.reshape(mesh.shape["layer"], 4, 8), ("layer", "unit_0", "unit_1"))
    return jax.shard_map(
        on_device,
        mesh=torus,
        in_specs=(
            P(),
            P(None, UNIT),
            P("layer", UNIT, None, None, None),
            P("layer", UNIT, None),
            P("layer", UNIT, None),
            P("layer", None, None, UNIT),
        ),
        out_specs=(
            P("layer", None, None, UNIT),
            P("layer", UNIT, None, None, None),
            P("layer", UNIT, None),
        ),
        check_vma=False,
    )
```

```python
import jax
import jax.numpy as jnp
from jax import lax
from jax.experimental import pallas as pl
from jax.experimental.pallas import tpu as pltpu
from jax.sharding import Mesh
from jax.sharding import PartitionSpec as P

UNIT = ("unit_0", "unit_1")
STREAMS = 1
LANES = 128
SPARE = 4
F32 = jnp.float32
BF16 = jnp.bfloat16
VMEM = pl.BlockSpec(memory_space=pltpu.VMEM)
SMEM = pl.BlockSpec(memory_space=pltpu.SMEM)
ANY = pl.BlockSpec(memory_space=pl.ANY)


def dot(lhs, rhs, dims):
    return lax.dot_general(lhs, rhs, (dims, ((), ())), preferred_element_type=F32)


def local(value):
    return pltpu.with_memory_space_constraint(value, pltpu.VMEM)


def like(value):
    return jax.ShapeDtypeStruct(value.shape, value.dtype)


def forward_kernel(own, nnz, blk, half_chunks, copies, first_row):
    def body(
        layout_ref, meta_ref, src_ref, hid_ref, w_ref, bias_ref, extra_ref, cell_in, _b, _c, _d,
        cell_ref, picked_ref, fac_ref, hlog_ref, send_ref, w_s, picked_s, w_sems, out_sems,
    ):
        fetches = [
            pltpu.make_async_copy(w_ref.at[j], w_s.at[j], w_sems.at[j]) for j in range(own)
        ]
        for fetch in fetches:
            fetch.start()
        active = meta_ref[0] > 0
        slot = meta_ref[1]
        started = meta_ref[2] > 0
        rows = src_ref.shape[1]
        mine = slice(first_row, first_row + rows)
        upper = lax.broadcasted_iota(jnp.int32, (rows, LANES), 1) >= blk

        def block(j, index, half):
            number = layout_ref[j * nnz + index]
            chunk = number // 2
            value = jnp.where(
                chunk < half_chunks,
                src_ref[jnp.minimum(chunk, half_chunks - 1)],
                hid_ref[jnp.maximum(chunk - half_chunks, 0)],
            )
            return jnp.where(number % 2 == half, value, pltpu.roll(value, blk, 1))

        sums = []
        stores = []
        for j in range(own):
            pairs = [
                jnp.where(upper, block(j, 2 * k + 1, 1), block(j, 2 * k, 0)) for k in range(nnz // 2)
            ]
            picked = jnp.concatenate(pairs, 1)
            picked_s[j] = picked
            place = picked_ref.at[slot, j, pl.ds(first_row, rows)]
            stores.append(pltpu.make_async_copy(picked_s.at[j], place, out_sems.at[j]))
            stores[j].start()
            fetches[j].wait()
            sums.append(dot(picked, w_s[j], ((1,), (0,))) + bias_ref[j])
        pre_act = jnp.concatenate(sums, 0)
        gates = jax.nn.sigmoid(pre_act)
        update = jnp.tanh(pre_act[:, 2 * blk : 3 * blk])
        in_gate = gates[:, :blk]
        forget = gates[:, blk : 2 * blk]
        out_gate = gates[:, 3 * blk :]
        cell_prev = jnp.where(started, cell_in[...], 0.0)
        cell = forget * cell_prev + in_gate * update
        squash = jnp.tanh(cell)
        cell_ref[...] = cell
        hidden = jnp.where(active, out_gate * squash, 0.0).astype(BF16)
        front = [update * in_gate * (1.0 - in_gate), cell_prev * forget * (1.0 - forget)]
        second = [in_gate * (1.0 - update * update), squash * out_gate * (1.0 - out_gate)]
        third = [out_gate * (1.0 - squash * squash), forget]
        factors = jnp.concatenate(front + second + third, 1)
        chunks = []
        for j in range(own):
            for column in range(fac_ref.shape[0]):
                first = j * rows + column * fac_ref.shape[3]
                fac_ref[column, slot, j] = factors[first : first + fac_ref.shape[3]]
        for c in range(own // 2):
            lanes = slice(c * LANES, (c + 1) * LANES)
            low = hidden[2 * c * rows : (2 * c + 1) * rows]
            high = hidden[(2 * c + 1) * rows : (2 * c + 2) * rows]
            joined = jnp.concatenate([low, high], 1)
            hlog_ref[slot, mine, lanes] = joined
            chunks.append(joined + extra_ref[meta_ref[3], mine, lanes])
        payload = jnp.concatenate(chunks, 0)
        for d in range(copies):
            send_ref[d] = payload
        for store in stores:
            store.wait()

    return body


def forward_call(layout, meta, src, hid, w, bias, extra, cell, logs, copies, stream):
    own, wide, _ = w.shape
    half_chunks, rows, _ = src.shape
    nnz = layout.shape[0] // own
    blk = wide // nnz
    send = jax.ShapeDtypeStruct((copies, own // 2 * rows, LANES), BF16)
    return pl.pallas_call(
        forward_kernel(own, nnz, blk, half_chunks, copies, stream * rows),
        in_specs=[SMEM, SMEM, VMEM, VMEM, ANY, VMEM, VMEM, VMEM, ANY, VMEM, VMEM],
        out_specs=[VMEM, ANY, VMEM, VMEM, VMEM],
        out_shape=[like(cell), *map(like, logs), send],
        scratch_shapes=[
            pltpu.VMEM(w.shape, w.dtype),
            pltpu.VMEM((own, rows, wide), BF16),
            pltpu.SemaphoreType.DMA((own,)),
            pltpu.SemaphoreType.DMA((own,)),
        ],
        input_output_aliases={7: 0, 8: 1, 9: 2, 10: 3},
        name="forward_wave",
    )(layout, meta, local(src), local(hid), w, bias, extra, local(cell), logs[0], local(logs[1]), local(logs[2]))


def backward_kernel(own, nnz, blk, half_chunks, columns, rows):
    part_width = 512
    group = half_chunks // columns

    def body(layout_ref, meta_ref, above_ref, recur_ref, cot_ref, fac_ref, carry_in, _p, *rest):
        w_refs, (carry_ref, pre_ref, sent_ref, acc, grad_s, w_s, w_sems) = (
            rest[:columns],
            rest[columns:],
        )
        fetches = [
            [
                pltpu.make_async_copy(w_refs[d].at[j], w_s.at[d, j], w_sems.at[d, j])
                for j in range(own)
            ]
            for d in range(columns)
        ]
        for several in fetches:
            for fetch in several:
                fetch.start()
        active = meta_ref[0] > 0
        slot = meta_ref[1]
        step = meta_ref[3]
        upper = lax.broadcasted_iota(jnp.int32, (rows, LANES), 1) >= blk
        acc[...] = jnp.zeros_like(acc)
        spare = acc.shape[0]
        total = above_ref[...].astype(F32) + cot_ref[step].astype(F32)
        for d in range(recur_ref.shape[0]):
            total = total + recur_ref[d, 1].astype(F32)
        grads = []
        for c in range(columns * own // 2):
            piece = total[c * rows : (c + 1) * rows]
            grads += [piece[:, :blk], piece[:, blk:]]
        grad_hidden = jnp.concatenate(grads, 0)
        factors = fac_ref[:, step].reshape(columns * own * rows, 3 * LANES)
        grad_cell = carry_in[...] + grad_hidden * factors[:, 2 * LANES : 2 * LANES + blk]
        carry_ref[...] = jnp.where(active, grad_cell * factors[:, 2 * LANES + blk :], 0.0)
        spread = jnp.concatenate([grad_cell, grad_cell, grad_cell, grad_hidden], 1)
        grad_all = jnp.where(active, spread * factors[:, : 2 * LANES], 0.0)
        for column in range(columns):
            for j in range(own):
                first = (column * own + j) * rows
                piece = grad_all[first : first + rows]
                grad_s[column * own + j] = piece
                pre_ref[column, slot, j] = piece.astype(BF16)
        for d in range(columns):
            column = lax.rem(meta_ref[4] + (columns - d), columns)
            for j in range(own):
                grad_pre = grad_s[column * own + j].astype(BF16)
                fetches[d][j].wait()
                for part in range(nnz * blk // part_width):
                    rows_w = slice(part * part_width, (part + 1) * part_width)
                    contrib = dot(grad_pre, w_s[d, j, rows_w, :], ((1,), (1,)))
                    for q in range(part_width // LANES):
                        value = contrib[:, q * LANES : (q + 1) * LANES]
                        swapped = pltpu.roll(value, blk, 1)
                        for half in range(2):
                            place = part * (part_width // blk) + 2 * q + half
                            number = layout_ref[(d * own + j) * nnz + place]
                            odd = number % 2
                            placed = jnp.where(odd == half, value, swapped)
                            placed = jnp.where(upper == (odd == 1), placed, 0.0)
                            acc[(2 * q + half) % spare, number // 2] += placed
        width = own // 2
        for z in range(sent_ref.shape[0]):
            for side in range(2):
                for column in range(columns):
                    first = side * half_chunks + column * group + z * width
                    value = acc[0, first : first + width]
                    for extra in range(1, spare):
                        value = value + acc[extra, first : first + width]
                    value = value.reshape(width * rows, LANES)
                    lines = slice(column * width * rows, (column + 1) * width * rows)
                    sent_ref[z, side, lines] = value.astype(BF16)

    return body


def backward_call(layout, meta, above, recur, cot, w_all, fac, carry, pre):
    columns = len(w_all)
    own, wide, gate_width = w_all[0].shape
    rows = pre.shape[3]
    nnz = layout.shape[0] // (own * columns)
    blk = wide // nnz
    half_chunks = recur.shape[0] * columns * own // 2
    return pl.pallas_call(
        backward_kernel(own, nnz, blk, half_chunks, columns, rows),
        in_specs=[SMEM, SMEM] + [VMEM] * 6 + [ANY] * columns,
        out_specs=[VMEM] * 3,
        out_shape=[like(carry), like(pre), like(recur)],
        scratch_shapes=[
            pltpu.VMEM((SPARE, 2 * half_chunks, rows, LANES), F32),
            pltpu.VMEM((columns * own, rows, gate_width), F32),
            pltpu.VMEM((columns, own, wide, gate_width), BF16),
            pltpu.SemaphoreType.DMA((columns, own)),
        ],
        input_output_aliases={6: 0, 7: 1},
        name="backward_wave",
    )(layout, meta, local(above), local(recur), cot, fac, local(carry), local(pre), *w_all)


def total_kernel(parts_ref, out_ref):
    total = parts_ref[0, 0].astype(F32)
    for d in range(1, parts_ref.shape[0]):
        total = total + parts_ref[d, 0].astype(F32)
    out_ref[...] = total.astype(BF16)


def total_of(parts):
    return pl.pallas_call(
        total_kernel,
        in_specs=[VMEM],
        out_specs=VMEM,
        out_shape=jax.ShapeDtypeStruct(parts.shape[2:], BF16),
        name="arrival_sum",
    )(local(parts))


def weight_grad_kernel(picked_ref, pre_ref, grad_ref, bias_ref):
    steps, _, rows, wide = picked_ref.shape
    columns = pre_ref.shape[0]
    lhs = picked_ref[...].reshape(steps * rows, wide)
    pieces = [pre_ref[c, t, 0].astype(F32) for t in range(steps) for c in range(columns)]
    rhs = jnp.concatenate(pieces, 0)
    grad_ref[0] = dot(lhs, rhs.astype(BF16), ((0,), (0,))).astype(BF16)
    bias_ref[0] = jnp.sum(rhs, 0, keepdims=True)


def weight_grads(picked, pre, steps):
    _, own, rows, wide = picked.shape
    columns, _, _, few, gate_width = pre.shape
    return pl.pallas_call(
        weight_grad_kernel,
        grid=(own,),
        in_specs=[
            pl.BlockSpec((steps, 1, rows, wide), lambda j: (0, j, 0, 0)),
            pl.BlockSpec((columns, steps, 1, few, gate_width), lambda j: (0, 0, j, 0, 0)),
        ],
        out_specs=[
            pl.BlockSpec((1, wide, gate_width), lambda j: (j, 0, 0)),
            pl.BlockSpec((1, 1, gate_width), lambda j: (j, 0, 0)),
        ],
        out_shape=[
            jax.ShapeDtypeStruct((own, wide, gate_width), BF16),
            jax.ShapeDtypeStruct((own, 1, gate_width), F32),
        ],
        name="weight_grads",
    )(picked, pre)


def exchanged(pieces):
    return lax.all_to_all(pieces, UNIT, 0, 0, tiled=True)


def on_device(tokens, embed, weights, layout, bias, d_hidden):
    layer_count = lax.axis_size("layer")
    layer_idx = lax.axis_index("layer")
    devices = lax.axis_size(UNIT)
    columns = lax.axis_size("unit_0")
    steps, batch = tokens.shape
    vocab, unit_width = embed.shape
    own, nnz, blk, gate_width = weights.shape[1:]
    w = weights[0].reshape(own, nnz * blk, gate_width)
    lay = layout[0].reshape(-1)
    bias_rows = bias[0].reshape(own, 1, gate_width)
    waves = steps + layer_count - 1
    rows = batch // STREAMS
    chunks = devices * own // 2
    few = batch // columns
    lay_all = [lay]
    w_rows = w.reshape(own * nnz * blk, gate_width)
    piece_rows = -(-w_rows.shape[0] // (16 * waves)) * 16
    moves = {}
    for turn in range(1, columns):
        moves[turn] = [(c, (c + turn) % columns) for c in range(columns)]
        lay_all.append(lax.ppermute(lay, "unit_0", moves[turn]))
    lay_all = jnp.concatenate(lay_all, 0)
    cot = d_hidden[0].reshape(steps, columns, few, unit_width).transpose(1, 0, 2, 3)
    cot = lax.all_to_all(cot, "unit_0", 0, 0, tiled=True)
    cot = cot.reshape(columns, steps, few, own // 2, LANES).transpose(1, 0, 3, 2, 4)
    cot = cot.reshape(steps, columns * own // 2 * few, LANES)

    vocab_ids = jnp.arange(vocab, dtype=jnp.int32)
    onehot = (tokens.reshape(-1)[:, None] == vocab_ids[None, :]).astype(BF16)
    looked = dot(onehot, embed, ((1,), (0,))).astype(BF16).reshape(steps, batch, unit_width)
    is_last = layer_idx == layer_count - 1
    looked = jnp.where(is_last, looked, jnp.zeros_like(looked))
    extra = jnp.concatenate([looked, jnp.zeros((1, batch, unit_width), BF16)], 0)
    ring = [(src, (src + 1) % layer_count) for src in range(layer_count)]
    lower = [(src, src - 1) for src in range(1, layer_count)]

    def meta_of(time_step, extra_row):
        in_range = (time_step >= 0) & (time_step < steps)
        clipped = jnp.clip(time_step, 0, steps - 1)
        slot = jnp.where(in_range, time_step, steps)
        later = in_range & (time_step > 0)
        row = clipped if extra_row is None else extra_row
        place = jnp.arange(5, dtype=jnp.int32)
        late = jnp.where(place == 2, later.astype(jnp.int32), row)
        late = jnp.where(place == 4, lax.axis_index("unit_0"), late)
        early = jnp.where(place == 0, in_range.astype(jnp.int32), slot)
        return jnp.where(place < 2, early, late)

    def forward_meta(wave):
        return meta_of(wave - layer_idx, jnp.minimum(wave + 1, steps))

    def backward_meta(wave):
        return meta_of(steps - 1 - wave + (layer_count - 1 - layer_idx), None)

    def first_payload(s):
        mine = extra[0, s * rows : (s + 1) * rows]
        flat = mine.reshape(rows, own // 2, LANES).transpose(1, 0, 2).reshape(-1, LANES)
        return jnp.broadcast_to(flat[None], (devices, *flat.shape))

    def gather(payload):
        return exchanged(payload).reshape(chunks, rows, LANES)

    def step(stream, meta, below, here, cell, logs):
        cell, *logs, send = forward_call(
            lay, meta, below, here, w, bias_rows, extra, cell, logs, devices, stream
        )
        return cell, logs, send

    def forward_wave(wave, state):
        meta, ready, held, cells, logs, others = state
        cells = list(cells)
        first = jnp.minimum(wave * piece_rows, w_rows.shape[0] - piece_rows)
        piece = lax.dynamic_slice(w_rows, (first, 0), (piece_rows, gate_width))
        new_others = []
        for turn, other in zip(moves, others):
            moved = lax.ppermute(piece, "unit_0", moves[turn])
            new_others.append(lax.dynamic_update_slice(other, moved, (first, 0)))
        last = STREAMS - 1
        for s in range(STREAMS):
            stream = (last + s) % STREAMS
            below = lax.ppermute(ready, "layer", ring)
            if STREAMS > 1:
                arriving = gather(held)
            if s == 0:
                following = forward_meta(wave + 1)
            cells[stream], logs, send = step(stream, meta, below, ready, cells[stream], logs)
            if STREAMS == 1:
                arriving = gather(send)
            ready, held = arriving, send
        return following, ready, held, tuple(cells), tuple(logs), tuple(new_others)

    logs = (
        jnp.zeros((steps + 1, own, batch, nnz * blk), BF16),
        jnp.zeros((columns, steps + 1, own, few, 3 * LANES), F32),
        jnp.zeros((steps + 1, batch, unit_width), BF16),
    )
    cells = tuple(jnp.zeros((own * rows, blk), F32) for _ in range(STREAMS))
    others = tuple(jnp.zeros(w_rows.shape, BF16) for _ in moves)
    sent_first = first_payload(0)
    start = (forward_meta(0), gather(sent_first), sent_first, cells, logs, others)
    (picked, fac, hlog), others = lax.fori_loop(0, waves, forward_wave, start)[-2:]
    w_all = [w, *[other.reshape(w.shape) for other in others]]

    fac = lax.all_to_all(fac, "unit_0", 0, 0, tiled=True)

    def backward_wave(wave, state):
        meta, above, recur, carry, pre = state
        carry, pre, sent = backward_call(lay_all, meta, above, recur, cot, w_all, fac, carry, pre)
        recur = lax.all_to_all(sent, "unit_1", 0, 0, tiled=True)
        following = backward_meta(wave + 1)
        down = total_of(recur)
        above = lax.ppermute(down, "layer", lower)
        return following, above, recur, carry, pre

    lines = columns * own // 2 * few
    start = (
        backward_meta(0),
        jnp.zeros((lines, LANES), BF16),
        jnp.zeros((devices // columns, 2, lines, LANES), BF16),
        jnp.zeros((columns * own * few, blk), F32),
        jnp.zeros((columns, steps + 1, own, few, gate_width), BF16),
    )
    pre = lax.fori_loop(0, waves, backward_wave, start)[-1]
    pre = lax.all_to_all(pre, "unit_0", 0, 0, tiled=True)
    grad_w, grad_b = weight_grads(picked, pre, steps)
    return (
        hlog[:steps][None],
        grad_w.reshape(1, own, nnz, blk, gate_width),
        grad_b.reshape(1, own, gate_width),
    )


def solution(mesh):
    torus = Mesh(mesh.devices.reshape(mesh.shape["layer"], 4, 8), ("layer", "unit_0", "unit_1"))
    return jax.shard_map(
        on_device,
        mesh=torus,
        in_specs=(
            P(),
            P(None, UNIT),
            P("layer", UNIT, None, None, None),
            P("layer", UNIT, None),
            P("layer", UNIT, None),
            P("layer", None, None, UNIT),
        ),
        out_specs=(
            P("layer", None, None, UNIT),
            P("layer", UNIT, None, None, None),
            P("layer", UNIT, None),
        ),
        check_vma=False,
    )
```

```python
import jax
import jax.numpy as jnp
from jax import lax
from jax.experimental import pallas as pl
from jax.experimental.pallas import tpu as pltpu
from jax.sharding import Mesh
from jax.sharding import PartitionSpec as P

UNIT = ("unit_0", "unit_1")
STREAMS = 1
LANES = 128
SPARE = 4
F32 = jnp.float32
BF16 = jnp.bfloat16
VMEM = pl.BlockSpec(memory_space=pltpu.VMEM)
SMEM = pl.BlockSpec(memory_space=pltpu.SMEM)
ANY = pl.BlockSpec(memory_space=pl.ANY)


def dot(lhs, rhs, dims):
    return lax.dot_general(lhs, rhs, (dims, ((), ())), preferred_element_type=F32)


def local(value):
    return pltpu.with_memory_space_constraint(value, pltpu.VMEM)


def unset(*shapes):
    return pl.pallas_call(
        lambda *refs: None,
        out_specs=[ANY] * len(shapes),
        out_shape=[jax.ShapeDtypeStruct(shape, BF16) for shape in shapes],
        name="unset",
    )()


def like(value):
    return jax.ShapeDtypeStruct(value.shape, value.dtype)


def forward_kernel(own, nnz, blk, half_chunks, copies, first_row):
    def body(
        layout_ref, meta_ref, src_ref, hid_ref, w_ref, bias_ref, extra_ref, cell_in, _b, _c, _d,
        cell_ref, picked_ref, fac_ref, hlog_ref, send_ref, w_s, picked_s, w_sems, out_sems,
    ):
        fetches = [
            pltpu.make_async_copy(w_ref.at[j], w_s.at[j], w_sems.at[j]) for j in range(own)
        ]
        for fetch in fetches:
            fetch.start()
        active = meta_ref[0] > 0
        slot = meta_ref[1]
        started = meta_ref[2] > 0
        rows = src_ref.shape[1]
        mine = slice(first_row, first_row + rows)
        upper = lax.broadcasted_iota(jnp.int32, (rows, LANES), 1) >= blk

        def block(j, index, half):
            number = layout_ref[j * nnz + index]
            chunk = number // 2
            value = jnp.where(
                chunk < half_chunks,
                src_ref[jnp.minimum(chunk, half_chunks - 1)],
                hid_ref[jnp.maximum(chunk - half_chunks, 0)],
            )
            return jnp.where(number % 2 == half, value, pltpu.roll(value, blk, 1))

        sums = []
        stores = []
        for j in range(own):
            pairs = [
                jnp.where(upper, block(j, 2 * k + 1, 1), block(j, 2 * k, 0)) for k in range(nnz // 2)
            ]
            picked = jnp.concatenate(pairs, 1)
            picked_s[j] = picked
            place = picked_ref.at[slot, j, pl.ds(first_row, rows)]
            stores.append(pltpu.make_async_copy(picked_s.at[j], place, out_sems.at[j]))
            stores[j].start()
            fetches[j].wait()
            sums.append(dot(picked, w_s[j], ((1,), (0,))) + bias_ref[j])
        pre_act = jnp.concatenate(sums, 0)
        gates = jax.nn.sigmoid(pre_act)
        update = jnp.tanh(pre_act[:, 2 * blk : 3 * blk])
        in_gate = gates[:, :blk]
        forget = gates[:, blk : 2 * blk]
        out_gate = gates[:, 3 * blk :]
        cell_prev = jnp.where(started, cell_in[...], 0.0)
        cell = forget * cell_prev + in_gate * update
        squash = jnp.tanh(cell)
        cell_ref[...] = cell
        hidden = jnp.where(active, out_gate * squash, 0.0).astype(BF16)
        front = [update * in_gate * (1.0 - in_gate), cell_prev * forget * (1.0 - forget)]
        second = [in_gate * (1.0 - update * update), squash * out_gate * (1.0 - out_gate)]
        third = [out_gate * (1.0 - squash * squash), forget]
        factors = jnp.concatenate(front + second + third, 1)
        chunks = []

        @pl.when(active)
        def _():
            for j in range(own):
                for column in range(fac_ref.shape[0]):
                    first = j * rows + column * fac_ref.shape[3]
                    fac_ref[column, slot, j] = factors[first : first + fac_ref.shape[3]]

        for c in range(own // 2):
            lanes = slice(c * LANES, (c + 1) * LANES)
            low = hidden[2 * c * rows : (2 * c + 1) * rows]
            high = hidden[(2 * c + 1) * rows : (2 * c + 2) * rows]
            joined = jnp.concatenate([low, high], 1)
            hlog_ref[slot, mine, lanes] = joined
            chunks.append(joined + extra_ref[meta_ref[3], mine, lanes])
        payload = jnp.concatenate(chunks, 0)
        for d in range(copies):
            send_ref[d] = payload
        for store in stores:
            store.wait()

    return body


def forward_call(layout, meta, src, hid, w, bias, extra, cell, logs, copies, stream):
    own, wide, _ = w.shape
    half_chunks, rows, _ = src.shape
    nnz = layout.shape[0] // own
    blk = wide // nnz
    send = pltpu.VMEM((copies, own // 2 * rows, LANES), BF16)
    return pl.pallas_call(
        forward_kernel(own, nnz, blk, half_chunks, copies, stream * rows),
        in_specs=[SMEM, SMEM, VMEM, VMEM, ANY, VMEM, VMEM, VMEM, ANY, VMEM, VMEM],
        out_specs=[VMEM, ANY, VMEM, VMEM, VMEM],
        out_shape=[like(cell), *map(like, logs), send],
        scratch_shapes=[
            pltpu.VMEM(w.shape, w.dtype),
            pltpu.VMEM((own, rows, wide), BF16),
            pltpu.SemaphoreType.DMA((own,)),
            pltpu.SemaphoreType.DMA((own,)),
        ],
        input_output_aliases={7: 0, 8: 1, 9: 2, 10: 3},
        name="forward_wave",
    )(layout, meta, local(src), local(hid), w, bias, extra, local(cell), logs[0], local(logs[1]), local(logs[2]))


def backward_kernel(own, nnz, blk, half_chunks, columns, rows):
    part_width = 512
    group = half_chunks // columns

    def body(layout_ref, meta_ref, above_ref, recur_ref, cot_ref, fac_ref, carry_in, _p, *rest):
        w_refs, (carry_ref, pre_ref, sent_ref, acc, grad_s, w_s, w_sems) = (
            rest[:columns],
            rest[columns:],
        )
        fetches = [
            [
                pltpu.make_async_copy(w_refs[d].at[j], w_s.at[d, j], w_sems.at[d, j])
                for j in range(own)
            ]
            for d in range(columns)
        ]
        for several in fetches:
            for fetch in several:
                fetch.start()
        active = meta_ref[0] > 0
        slot = meta_ref[1]
        step = meta_ref[3]
        upper = lax.broadcasted_iota(jnp.int32, (rows, LANES), 1) >= blk
        acc[...] = jnp.zeros_like(acc)
        spare = acc.shape[0]
        total = above_ref[...].astype(F32) + cot_ref[step].astype(F32)
        for d in range(recur_ref.shape[0]):
            total = total + recur_ref[d, 1].astype(F32)
        grads = []
        for c in range(columns * own // 2):
            piece = total[c * rows : (c + 1) * rows]
            grads += [piece[:, :blk], piece[:, blk:]]
        grad_hidden = jnp.concatenate(grads, 0)
        factors = fac_ref[:, step].reshape(columns * own * rows, 3 * LANES)
        grad_cell = carry_in[...] + grad_hidden * factors[:, 2 * LANES : 2 * LANES + blk]
        carry_ref[...] = jnp.where(active, grad_cell * factors[:, 2 * LANES + blk :], 0.0)
        spread = jnp.concatenate([grad_cell, grad_cell, grad_cell, grad_hidden], 1)
        grad_all = jnp.where(active, spread * factors[:, : 2 * LANES], 0.0)
        for column in range(columns):
            for j in range(own):
                first = (column * own + j) * rows
                piece = grad_all[first : first + rows]
                grad_s[column * own + j] = piece
                pre_ref[column, slot, j] = piece.astype(BF16)
        for d in range(columns):
            column = lax.rem(meta_ref[4] + (columns - d), columns)
            for j in range(own):
                grad_pre = grad_s[column * own + j].astype(BF16)
                fetches[d][j].wait()
                for part in range(nnz * blk // part_width):
                    rows_w = slice(part * part_width, (part + 1) * part_width)
                    contrib = dot(grad_pre, w_s[d, j, rows_w, :], ((1,), (1,)))
                    for q in range(part_width // LANES):
                        value = contrib[:, q * LANES : (q + 1) * LANES]
                        swapped = pltpu.roll(value, blk, 1)
                        for half in range(2):
                            place = part * (part_width // blk) + 2 * q + half
                            number = layout_ref[(d * own + j) * nnz + place]
                            odd = number % 2
                            placed = jnp.where(odd == half, value, swapped)
                            placed = jnp.where(upper == (odd == 1), placed, 0.0)
                            acc[(2 * q + half) % spare, number // 2] += placed
        width = own // 2
        for z in range(sent_ref.shape[0]):
            for side in range(2):
                for column in range(columns):
                    first = side * half_chunks + column * group + z * width
                    value = acc[0, first : first + width]
                    for extra in range(1, spare):
                        value = value + acc[extra, first : first + width]
                    value = value.reshape(width * rows, LANES)
                    lines = slice(column * width * rows, (column + 1) * width * rows)
                    sent_ref[z, side, lines] = value.astype(BF16)

    return body


def backward_call(layout, meta, above, recur, cot, w_all, fac, carry, pre):
    columns = len(w_all)
    own, wide, gate_width = w_all[0].shape
    rows = pre.shape[3]
    nnz = layout.shape[0] // (own * columns)
    blk = wide // nnz
    half_chunks = recur.shape[0] * columns * own // 2
    return pl.pallas_call(
        backward_kernel(own, nnz, blk, half_chunks, columns, rows),
        in_specs=[SMEM, SMEM] + [VMEM] * 6 + [ANY] * columns,
        out_specs=[VMEM] * 3,
        out_shape=[like(carry), like(pre), pltpu.VMEM(recur.shape, recur.dtype)],
        scratch_shapes=[
            pltpu.VMEM((SPARE, 2 * half_chunks, rows, LANES), F32),
            pltpu.VMEM((columns * own, rows, gate_width), F32),
            pltpu.VMEM((columns, own, wide, gate_width), BF16),
            pltpu.SemaphoreType.DMA((columns, own)),
        ],
        input_output_aliases={6: 0, 7: 1},
        name="backward_wave",
    )(layout, meta, local(above), local(recur), cot, fac, local(carry), local(pre), *w_all)


def total_kernel(parts_ref, out_ref):
    total = parts_ref[0, 0].astype(F32)
    for d in range(1, parts_ref.shape[0]):
        total = total + parts_ref[d, 0].astype(F32)
    out_ref[...] = total.astype(BF16)


def total_of(parts):
    return pl.pallas_call(
        total_kernel,
        in_specs=[VMEM],
        out_specs=VMEM,
        out_shape=jax.ShapeDtypeStruct(parts.shape[2:], BF16),
        name="arrival_sum",
    )(local(parts))


def weight_grad_kernel(picked_ref, pre_ref, grad_ref, bias_ref):
    steps, _, rows, wide = picked_ref.shape
    columns = pre_ref.shape[0]
    lhs = picked_ref[...].reshape(steps * rows, wide)
    pieces = [pre_ref[c, t, 0].astype(F32) for t in range(steps) for c in range(columns)]
    rhs = jnp.concatenate(pieces, 0)
    grad_ref[0] = dot(lhs, rhs.astype(BF16), ((0,), (0,))).astype(BF16)
    bias_ref[pl.ds(pl.program_id(0), 1)] = jnp.sum(rhs, 0, keepdims=True)


def weight_grads(picked, pre, steps):
    _, own, rows, wide = picked.shape
    columns, _, _, few, gate_width = pre.shape
    return pl.pallas_call(
        weight_grad_kernel,
        grid=(own,),
        in_specs=[
            pl.BlockSpec((steps, 1, rows, wide), lambda j: (0, j, 0, 0)),
            pl.BlockSpec((columns, steps, 1, few, gate_width), lambda j: (0, 0, j, 0, 0)),
        ],
        out_specs=[
            pl.BlockSpec((1, wide, gate_width), lambda j: (j, 0, 0)),
            pl.BlockSpec((own, gate_width), lambda j: (0, 0)),
        ],
        out_shape=[
            jax.ShapeDtypeStruct((own, wide, gate_width), BF16),
            jax.ShapeDtypeStruct((own, gate_width), F32),
        ],
        name="weight_grads",
    )(picked, pre)


def exchanged(pieces):
    return lax.all_to_all(pieces, UNIT, 0, 0, tiled=True)


def on_device(tokens, embed, weights, layout, bias, d_hidden):
    layer_count = lax.axis_size("layer")
    layer_idx = lax.axis_index("layer")
    devices = lax.axis_size(UNIT)
    columns = lax.axis_size("unit_0")
    steps, batch = tokens.shape
    vocab, unit_width = embed.shape
    own, nnz, blk, gate_width = weights.shape[1:]
    w = weights[0].reshape(own, nnz * blk, gate_width)
    lay = layout[0].reshape(-1)
    bias_rows = bias[0].reshape(own, 1, gate_width)
    waves = steps + layer_count - 1
    rows = batch // STREAMS
    chunks = devices * own // 2
    few = batch // columns
    lay_all = [lay]
    w_rows = w.reshape(own * nnz * blk, gate_width)
    piece_rows = -(-w_rows.shape[0] // (16 * waves)) * 16
    moves = {}
    for turn in range(1, columns):
        moves[turn] = [(c, (c + turn) % columns) for c in range(columns)]
        lay_all.append(lax.ppermute(lay, "unit_0", moves[turn]))
    lay_all = jnp.concatenate(lay_all, 0)
    cot = d_hidden[0].reshape(steps, columns, few, unit_width).transpose(1, 0, 2, 3)
    cot = lax.all_to_all(cot, "unit_0", 0, 0, tiled=True)
    cot = cot.reshape(columns, steps, few, own // 2, LANES).transpose(1, 0, 3, 2, 4)
    cot = cot.reshape(steps, columns * own // 2 * few, LANES)

    vocab_ids = jnp.arange(vocab, dtype=jnp.int32)
    onehot = (tokens.reshape(-1)[:, None] == vocab_ids[None, :]).astype(BF16)
    looked = dot(onehot, embed, ((1,), (0,))).astype(BF16).reshape(steps, batch, unit_width)
    is_last = layer_idx == layer_count - 1
    looked = jnp.where(is_last, looked, jnp.zeros_like(looked))
    extra = jnp.concatenate([looked, jnp.zeros((1, batch, unit_width), BF16)], 0)
    ring = [(src, (src + 1) % layer_count) for src in range(layer_count)]
    lower = [(src, src - 1) for src in range(1, layer_count)]

    def meta_of(time_step, extra_row):
        in_range = (time_step >= 0) & (time_step < steps)
        clipped = jnp.clip(time_step, 0, steps - 1)
        slot = jnp.where(in_range, time_step, steps)
        later = in_range & (time_step > 0)
        row = clipped if extra_row is None else extra_row
        place = jnp.arange(5, dtype=jnp.int32)
        late = jnp.where(place == 2, later.astype(jnp.int32), row)
        late = jnp.where(place == 4, lax.axis_index("unit_0"), late)
        early = jnp.where(place == 0, in_range.astype(jnp.int32), slot)
        return jnp.where(place < 2, early, late)

    def forward_meta(wave):
        return meta_of(wave - layer_idx, jnp.minimum(wave + 1, steps))

    def backward_meta(wave):
        return meta_of(steps - 1 - wave + (layer_count - 1 - layer_idx), None)

    def first_payload(s):
        mine = extra[0, s * rows : (s + 1) * rows]
        flat = mine.reshape(rows, own // 2, LANES).transpose(1, 0, 2).reshape(-1, LANES)
        return jnp.broadcast_to(flat[None], (devices, *flat.shape))

    def gather(payload):
        return exchanged(payload).reshape(chunks, rows, LANES)

    def step(stream, meta, below, here, cell, logs):
        cell, *logs, send = forward_call(
            lay, meta, below, here, w, bias_rows, extra, cell, logs, devices, stream
        )
        return cell, logs, send

    def forward_wave(wave, state):
        meta, ready, held, cells, logs, others = state
        cells = list(cells)
        first = jnp.minimum(wave * piece_rows, w_rows.shape[0] - piece_rows)
        piece = lax.dynamic_slice(w_rows, (first, 0), (piece_rows, gate_width))
        new_others = []
        for turn, other in zip(moves, others):
            moved = lax.ppermute(piece, "unit_0", moves[turn])
            new_others.append(lax.dynamic_update_slice(other, moved, (first, 0)))
        last = STREAMS - 1
        for s in range(STREAMS):
            stream = (last + s) % STREAMS
            below = lax.ppermute(ready, "layer", ring)
            if STREAMS > 1:
                arriving = gather(held)
            if s == 0:
                following = forward_meta(wave + 1)
            cells[stream], logs, send = step(stream, meta, below, ready, cells[stream], logs)
            if STREAMS == 1:
                arriving = gather(send)
            ready, held = arriving, send
        return following, ready, held, tuple(cells), tuple(logs), tuple(new_others)

    picked, *others = unset(
        (steps + 1, own, batch, nnz * blk), *[w_rows.shape for _ in moves]
    )
    logs = (
        picked,
        jnp.zeros((columns, steps, own, few, 3 * LANES), F32),
        jnp.zeros((steps + 1, batch, unit_width), BF16),
    )
    cells = tuple(jnp.zeros((own * rows, blk), F32) for _ in range(STREAMS))
    sent_first = first_payload(0)
    start = (forward_meta(0), gather(sent_first), sent_first, cells, logs, tuple(others))
    (picked, fac, hlog), others = lax.fori_loop(0, waves, forward_wave, start)[-2:]
    w_all = [w, *[other.reshape(w.shape) for other in others]]

    fac = lax.all_to_all(fac, "unit_0", 0, 0, tiled=True)

    def backward_wave(wave, state):
        meta, above, recur, carry, pre = state
        carry, pre, sent = backward_call(lay_all, meta, above, recur, cot, w_all, fac, carry, pre)
        recur = lax.all_to_all(sent, "unit_1", 0, 0, tiled=True)
        following = backward_meta(wave + 1)
        down = total_of(recur)
        above = lax.ppermute(down, "layer", lower)
        return following, above, recur, carry, pre

    lines = columns * own // 2 * few
    start = (
        backward_meta(0),
        jnp.zeros((lines, LANES), BF16),
        jnp.zeros((devices // columns, 2, lines, LANES), BF16),
        jnp.zeros((columns * own * few, blk), F32),
        jnp.zeros((columns, steps + 1, own, few, gate_width), BF16),
    )
    pre = lax.fori_loop(0, waves, backward_wave, start)[-1]
    pre = lax.all_to_all(pre, "unit_0", 0, 0, tiled=True)
    grad_w, grad_b = weight_grads(picked, pre, steps)
    return (
        hlog[:steps][None],
        grad_w.reshape(1, own, nnz, blk, gate_width),
        grad_b.reshape(1, own, gate_width),
    )


def solution(mesh):
    torus = Mesh(mesh.devices.reshape(mesh.shape["layer"], 4, 8), ("layer", "unit_0", "unit_1"))
    return jax.shard_map(
        on_device,
        mesh=torus,
        in_specs=(
            P(),
            P(None, UNIT),
            P("layer", UNIT, None, None, None),
            P("layer", UNIT, None),
            P("layer", UNIT, None),
            P("layer", None, None, UNIT),
        ),
        out_specs=(
            P("layer", None, None, UNIT),
            P("layer", UNIT, None, None, None),
            P("layer", UNIT, None),
        ),
        check_vma=False,
    )
```
